128 devices in a mesh: el: 8 (over x, core), tg: 16 (over y, z).
Axes of the slice: x: 4, y: 4, z: 4, core: 2. Of those that a mesh axis runs over, the one named last changes fastest.
Arguments:
- field_points: bfloat16 [65536, 16, 256], P(('el', 'tg')), may hold values from -6 to 6
- owner_map: int32 [128, 512], P(('el', 'tg')), may hold values from 0 to 127, as said below
- send_counts: int32 [128, 512], P(('el', 'tg')), may hold values from 15 to 16
- tile_rows: int32 [128, 32], P(('el', 'tg')), may hold values from 0 to 31, each once within a row
- tile_cols: int32 [128, 32, 16], P(('el', 'tg')), may hold values from 0 to 63, as said below
- weights: bfloat16 [128, 32, 16, 128, 128], P(('el', 'tg')), may hold values from -0.125 to 0.125
Outputs:
- remapped: bfloat16 [256, 524288], P('el', 'tg')
The draws below stay inside these ranges and needn't reach their ends.
Inputs may be any that keep to these rules, and one draw needn't show every extreme that they name: `owner_map`: each device's 512 elements name every owner exactly 4 times. `tile_cols`: the 16 entries of one target tile are distinct.
All inputs are finite; a program needn't handle non-finite values.
Results may differ from the reference program's by a relative error of at most 0.001.
Values may be sent and summed in bfloat16 or wider, within the bound.
No kernel may reach another device: no remote copies, remote signals or barrier semaphores. Data moves between devices by JAX's collectives and lax.ppermute only.
A program may use at most 128 MiB of HBM per device.

```python
import jax
import jax.numpy as jnp
from jax import lax

NPTS = 16
TILE = 128
BLOCKS = 16
ELEM_DEV = 512
TTILES = 32
CH = 256
PER_OWNER = 4
LOCAL_TILES = 64
ELEMS = 65536
TGT_ROWS = 524288
N_EL = 8
N_TG = 16
DEVICES = 128


def owner_table(key):
    keys = jax.random.split(jax.random.fold_in(key, 11), DEVICES)
    shuffled = jax.vmap(lambda single: jax.random.permutation(single, ELEM_DEV))(keys)
    return (shuffled % DEVICES).astype(jnp.int32)


def draw_owner_map(key, part):
    return owner_table(key)


def draw_send_counts(key, part):
    owners = owner_table(key)
    full_owner = jax.random.randint(jax.random.fold_in(key, 12), (DEVICES,), 0, DEVICES)
    base_counts = jax.random.randint(jax.random.fold_in(key, 13), (DEVICES, ELEM_DEV), 15, NPTS + 1)
    return jnp.where(owners == full_owner[:, None], NPTS, base_counts).astype(jnp.int32)


def draw_tile_cols(key, part):
    keys = jax.random.split(jax.random.fold_in(key, 14), DEVICES * TTILES)
    picks = jax.vmap(lambda single: jax.random.permutation(single, LOCAL_TILES)[:BLOCKS])(keys)
    return picks.reshape(DEVICES, TTILES, BLOCKS).astype(jnp.int32)


def shard_levels(key, dims, cuts, smallest, high):
    gain = 1.0
    for dim, shards_of in cuts:
        steps = jax.random.uniform(jax.random.fold_in(jax.random.fold_in(key, 6), dim), (shards_of,), jnp.float32, smallest / len(cuts), high / len(cuts))
        gain = gain * jnp.repeat(jnp.exp(steps), dims[dim] // shards_of).reshape((-1,) + (1,) * (len(dims) - 1 - dim))
    return gain


def centred(rng, extent, spread, limit, shards=(), kind=jnp.bfloat16):
    values = jax.random.normal(rng, extent, jnp.float32) * spread
    if len(shards) > 0:
        values = shard_levels(rng, extent, shards, -0.22, 0.18) * values
    return jnp.clip(values, min=-limit, max=limit).astype(kind)


def setup_inputs(seed: int = 0) -> dict:
    seeds = jax.random.split(jax.random.key(seed), 7)
    return {
        "field_points": centred(seeds[0], (ELEMS, NPTS, CH), 1.0, 6.0, ((0, 128),)),
        "owner_map": draw_owner_map(jax.random.fold_in(seeds[6], 71), 0),
        "send_counts": draw_send_counts(jax.random.fold_in(seeds[6], 71), 0),
        "tile_rows": jax.vmap(lambda own: jax.random.permutation(own, TTILES))(jax.random.split(seeds[3], DEVICES)).reshape((DEVICES, TTILES)).astype(jnp.int32),
        "tile_cols": draw_tile_cols(jax.random.fold_in(seeds[6], 71), 0),
        "weights": centred(seeds[5], (DEVICES, TTILES, BLOCKS, TILE, TILE), (BLOCKS * TILE) ** -0.5, 0.125, ((0, 128),)),
    }


def reference(field_points, owner_map, send_counts, tile_rows, tile_cols, weights):
    device_total = N_EL * N_TG
    ordering = jnp.argsort(owner_map, axis=1, stable=True).astype(jnp.int32)
    selected = ordering.reshape(device_total, device_total, PER_OWNER)
    offsets = (jnp.arange(device_total).astype(jnp.int32) * ELEM_DEV).astype(jnp.int32)
    global_ids = (selected + offsets[:, None, None]).astype(jnp.int32)
    flat_counts = send_counts.reshape(-1)
    point_index = jnp.arange(NPTS).astype(jnp.int32)

    def owner_work(owner):
        ids = global_ids[:, owner, :].reshape(-1)
        rows = field_points[ids]
        live_rows = point_index[None, :] < flat_counts[ids][:, None]
        rows = jnp.where(live_rows[:, :, None], rows, jnp.zeros((), rows.dtype))
        source = rows.reshape(LOCAL_TILES, TILE, CH)
        gathered = source[tile_cols[owner]].astype(jnp.float32)
        product = jnp.einsum("tkij,tkjc->cti", weights[owner].astype(jnp.float32), gathered)
        placed = jnp.zeros_like(product).at[:, tile_rows[owner]].set(product)
        return placed.reshape(CH, TTILES * TILE).astype(jnp.bfloat16)

    results = lax.map(owner_work, jnp.arange(device_total).astype(jnp.int32))
    results = results.reshape(N_EL, N_TG, CH, TTILES * TILE)
    return results.transpose(2, 1, 0, 3).reshape(CH, TGT_ROWS)
```

```python
import functools
import jax
import jax.numpy as jnp
from jax import lax
from jax.experimental import pallas as pl
from jax.experimental.pallas import tpu as pltpu
from jax.sharding import PartitionSpec as P


def pack_kernel(chunks, owner_ref, counts_ref, field_ref, out_ref, buf, dst, pos_v, pos_s, sem_in, sem_pos, sem_out):
    elems, points, channels = dst.shape
    step = elems // chunks
    owners = elems // 4
    def fetch(c):
        return pltpu.make_async_copy(field_ref.at[pl.ds(c * step, step)], buf.at[pl.ds(c * step, step)], sem_in.at[c])
    for c in range(chunks):
        fetch(c).start()
    owner = owner_ref[...]
    hit = lax.broadcasted_iota(jnp.int32, (owners, elems), 0) == owner
    hit = jnp.where(hit, 1.0, 0.0)
    before = jnp.where(lax.broadcasted_iota(jnp.int32, (elems, elems), 0) < lax.broadcasted_iota(jnp.int32, (elems, elems), 1), 1.0, 0.0)
    earlier = jnp.dot(hit.astype(jnp.bfloat16), before.astype(jnp.bfloat16), preferred_element_type=jnp.float32)
    rank = jnp.sum(hit * earlier, axis=0, keepdims=True)
    pos_v[...] = owner * 4 + rank.astype(jnp.int32)
    cp = pltpu.make_async_copy(pos_v, pos_s, sem_pos)
    cp.start()
    cp.wait()
    point = lax.broadcasted_iota(jnp.int32, (points, channels), 0)
    for c in range(chunks):
        fetch(c).wait()
        def body(e, carry):
            live = point < counts_ref[0, e]
            dst[pos_s[0, e]] = jnp.where(live, buf[e], jnp.zeros((), buf.dtype))
            return carry
        lax.fori_loop(c * step, (c + 1) * step, body, 0, unroll=8)
    out = pltpu.make_async_copy(dst, out_ref, sem_out)
    out.start()
    out.wait()

def pack(owner_map, send_counts, field, chunks=8):
    return pl.pallas_call(
        functools.partial(pack_kernel, chunks),
        out_shape=jax.ShapeDtypeStruct(field.shape, field.dtype),
        in_specs=[pl.BlockSpec(memory_space=pltpu.VMEM), pl.BlockSpec(memory_space=pltpu.SMEM), pl.BlockSpec(memory_space=pl.ANY)],
        out_specs=pl.BlockSpec(memory_space=pl.ANY),
        scratch_shapes=[
            pltpu.VMEM(field.shape, field.dtype),
            pltpu.VMEM(field.shape, field.dtype),
            pltpu.VMEM((1, field.shape[0]), jnp.int32),
            pltpu.SMEM((1, field.shape[0]), jnp.int32),
            pltpu.SemaphoreType.DMA((chunks,)),
            pltpu.SemaphoreType.DMA,
            pltpu.SemaphoreType.DMA,
        ],
        name="pack",
    )(owner_map, send_counts, field)

def remap_kernel(rows_ref, cols_ref, w_ref, src_ref, out_ref):
    t = pl.program_id(0)
    per, blocks, tile, _ = w_ref.shape[1:]
    for u in range(per):
        tt = t * per + u
        acc = None
        for k in range(0, blocks, 2):
            w = jnp.concatenate([w_ref[0, u, k], w_ref[0, u, k + 1]], axis=1)
            s = jnp.concatenate([src_ref[cols_ref[0, tt, k]], src_ref[cols_ref[0, tt, k + 1]]], axis=0)
            p = jnp.dot(w, s, preferred_element_type=jnp.float32)
            acc = p if acc is None else acc + p
        lane = pl.multiple_of(rows_ref[0, tt] * tile, tile)
        out_ref[:, pl.ds(lane, tile)] = acc.T.astype(out_ref.dtype)

def remap(tile_rows, tile_cols, weights, source, per=1):
    _, targets, blocks, tile, _ = weights.shape
    channels = source.shape[-1]
    return pl.pallas_call(
        remap_kernel,
        out_shape=jax.ShapeDtypeStruct((channels, targets * tile), jnp.bfloat16),
        grid_spec=pltpu.PrefetchScalarGridSpec(
            num_scalar_prefetch=2,
            grid=(targets // per,),
            in_specs=[
                pl.BlockSpec((1, per, blocks, tile, tile), lambda t, *_: (0, t, 0, 0, 0)),
                pl.BlockSpec(source.shape, lambda t, *_: (0, 0, 0)),
            ],
            out_specs=pl.BlockSpec((channels, targets * tile), lambda t, *_: (0, 0)),
        ),
        name="remap",
    )(tile_rows, tile_cols, weights, source)


def on_device(field_points, owner_map, send_counts, tile_rows, tile_cols, weights):
    elems, points, channels = field_points.shape
    devices = lax.axis_size(("el", "tg"))
    packed = pack(owner_map, send_counts, field_points)
    outgoing = packed.reshape(devices, elems // devices * points, channels)
    incoming = lax.all_to_all(outgoing, ("el", "tg"), split_axis=0, concat_axis=0, tiled=True)
    source = incoming.reshape(-1, weights.shape[-1], channels)
    merged = remap(tile_rows, tile_cols, weights, source, per=8)
    return lax.all_to_all(merged, "el", split_axis=0, concat_axis=1, tiled=True)


def solution(mesh):
    return jax.shard_map(
        on_device,
        mesh=mesh,
        in_specs=(
            P(("el", "tg"), None, None),
            P(("el", "tg"), None),
            P(("el", "tg"), None),
            P(("el", "tg"), None),
            P(("el", "tg"), None, None),
            P(("el", "tg"), None, None, None, None),
        ),
        out_specs=P("el", "tg"),
        check_vma=False,
    )
```

```python
import functools

import jax
import jax.numpy as jnp
from jax import lax
from jax.experimental import pallas as pl
from jax.experimental.pallas import tpu as pltpu
from jax.sharding import PartitionSpec as P

PARTS = 2
HOPS = ((2, 0), (2, 1), (1, 0), (3, 0), (1, 1), (3, 1), (0, 1), (0, 0))


def pack_kernel(chunks, owner_ref, counts_ref, field_ref, out_ref, buf, dst, pos_v, pos_s, sem_in, sem_pos, sem_out):
    elems, points, channels = dst.shape
    step = elems // chunks
    owners = elems // 4

    def fetch(c):
        return pltpu.make_async_copy(field_ref.at[pl.ds(c * step, step)], buf.at[pl.ds(c * step, step)], sem_in.at[c])

    for c in range(chunks):
        fetch(c).start()
    owner = owner_ref[...]
    hit = lax.broadcasted_iota(jnp.int32, (owners, elems), 0) == owner
    hit = jnp.where(hit, 1.0, 0.0)
    before = jnp.where(lax.broadcasted_iota(jnp.int32, (elems, elems), 0) < lax.broadcasted_iota(jnp.int32, (elems, elems), 1), 1.0, 0.0)
    earlier = jnp.dot(hit.astype(jnp.bfloat16), before.astype(jnp.bfloat16), preferred_element_type=jnp.float32)
    rank = jnp.sum(hit * earlier, axis=0, keepdims=True)
    pos_v[...] = owner * 4 + rank.astype(jnp.int32)
    cp = pltpu.make_async_copy(pos_v, pos_s, sem_pos)
    cp.start()
    cp.wait()
    point = lax.broadcasted_iota(jnp.int32, (points, channels), 0)
    for c in range(chunks):
        fetch(c).wait()

        def body(e, carry):
            live = point < counts_ref[0, e]
            dst[pos_s[0, e]] = jnp.where(live, buf[e], jnp.zeros((), buf.dtype))
            return carry

        lax.fori_loop(c * step, (c + 1) * step, body, 0, unroll=8)
    out = pltpu.make_async_copy(dst, out_ref, sem_out)
    out.start()
    out.wait()


def pack(owner_map, send_counts, field, chunks=8):
    return pl.pallas_call(
        functools.partial(pack_kernel, chunks),
        out_shape=jax.ShapeDtypeStruct(field.shape, field.dtype),
        in_specs=[pl.BlockSpec(memory_space=pltpu.VMEM), pl.BlockSpec(memory_space=pltpu.SMEM), pl.BlockSpec(memory_space=pl.ANY)],
        out_specs=pl.BlockSpec(memory_space=pl.ANY),
        scratch_shapes=[
            pltpu.VMEM(field.shape, field.dtype),
            pltpu.VMEM(field.shape, field.dtype),
            pltpu.VMEM((1, field.shape[0]), jnp.int32),
            pltpu.SMEM((1, field.shape[0]), jnp.int32),
            pltpu.SemaphoreType.DMA((chunks,)),
            pltpu.SemaphoreType.DMA,
            pltpu.SemaphoreType.DMA,
        ],
        name="pack",
    )(owner_map, send_counts, field)


def peer(me, groups, hop):
    chip, core = me // 2, me % 2
    return lax.rem(chip + hop[0], groups // 2) * 2 + (1 - core if hop[1] else core)


def remap_kernel(part, lag, axis, rows_ref, cols_ref, w_ref, src_ref, *refs):
    outs, (w_buf, src, out, order, sem_src, sem_w) = refs[: len(HOPS)], refs[len(HOPS) :]
    _, targets, blocks, tile, _ = w_ref.shape
    count = w_buf.shape[0]
    me = lax.axis_index(axis) if axis else 0
    groups = len(HOPS)
    rows = out.shape[0] // groups
    load = pltpu.make_async_copy(src_ref, src, sem_src)
    load.start()
    for t in range(targets):
        order[rows_ref[0, t]] = t

    def fetch(q):
        return pltpu.make_async_copy(w_ref.at[0, order[part * count + q]], w_buf.at[q], sem_w.at[q])

    for q in range(count):
        fetch(q).start()
    load.wait()

    def body(s, carry):
        for u in range(lag):
            q = s * lag + u
            t = order[part * count + q]
            fetch(q).wait()
            w = jnp.concatenate([w_buf[q, k] for k in range(blocks)], axis=1)
            x = jnp.concatenate([src[cols_ref[0, t, k]] for k in range(blocks)], axis=0)
            r = jnp.dot(w, x, preferred_element_type=jnp.float32)
            out[:, pl.ds(pl.multiple_of(q * tile, tile), tile)] = r.T.astype(out.dtype)
        return carry

    lax.fori_loop(0, count // lag, body, 0)
    for i, hop in enumerate(HOPS):
        row = pl.multiple_of(peer(me, groups, hop) * rows, rows)
        outs[i][...] = out[pl.ds(row, rows)]


def remap(part, tile_rows, tile_cols, weights, source, lag=2, axis="el"):
    _, targets, blocks, tile, _ = weights.shape
    channels = source.shape[-1]
    count = targets // PARTS
    piece = jax.ShapeDtypeStruct((channels // len(HOPS), count * tile), source.dtype)
    return pl.pallas_call(
        functools.partial(remap_kernel, part, lag, axis),
        out_shape=[piece] * len(HOPS),
        in_specs=[pl.BlockSpec(memory_space=pltpu.SMEM)] * 2 + [pl.BlockSpec(memory_space=pl.ANY)] * 2,
        out_specs=[pl.BlockSpec(memory_space=pltpu.VMEM)] * len(HOPS),
        scratch_shapes=[
            pltpu.VMEM((count, *weights.shape[2:]), weights.dtype),
            pltpu.VMEM(source.shape, source.dtype),
            pltpu.VMEM((channels, count * tile), source.dtype),
            pltpu.SMEM((targets,), jnp.int32),
            pltpu.SemaphoreType.DMA,
            pltpu.SemaphoreType.DMA((count,)),
        ],
        compiler_params=pltpu.CompilerParams(vmem_limit_bytes=46 << 20),
        cost_estimate=pl.CostEstimate(
            flops=2 * count * blocks * tile * tile * channels,
            bytes_accessed=2 * (weights.size // PARTS + source.size),
            transcendentals=0,
        ),
    )(tile_rows, tile_cols, weights, source)


def join_kernel(part, axis, *refs):
    pieces, (out_ref, sems) = refs[: len(HOPS)], refs[-2:]
    me = lax.axis_index(axis) if axis else 0
    groups = len(HOPS)
    width = pieces[0].shape[1]
    stores = []
    for i, (chip, core) in enumerate(HOPS):
        source = peer(me, groups, ((groups // 2 - chip) % (groups // 2), core))
        lane = pl.multiple_of((source * PARTS + part) * width, width)
        stores.append(pltpu.make_async_copy(pieces[i], out_ref.at[:, pl.ds(lane, width)], sems.at[i]))
        stores[i].start()
    for store in stores:
        store.wait()


def join(part, pieces, whole=None, axis="el"):
    rows, width = pieces[0].shape
    groups = len(HOPS)
    kept = [] if whole is None else [whole]
    return pl.pallas_call(
        functools.partial(join_kernel, part, axis),
        out_shape=jax.ShapeDtypeStruct((rows, groups * PARTS * width), pieces[0].dtype),
        in_specs=[pl.BlockSpec(memory_space=pltpu.VMEM)] * groups + [pl.BlockSpec(memory_space=pl.ANY)] * len(kept),
        out_specs=pl.BlockSpec(memory_space=pl.ANY),
        scratch_shapes=[pltpu.SemaphoreType.DMA((groups,))],
        input_output_aliases={groups: 0} if kept else {},
        compiler_params=pltpu.CompilerParams(vmem_limit_bytes=8 << 20),
        cost_estimate=pl.CostEstimate(flops=0, bytes_accessed=4 * groups * rows * width, transcendentals=0),
    )(*pieces, *kept)


def on_device(field_points, owner_map, send_counts, tile_rows, tile_cols, weights):
    elems, points, channels = field_points.shape
    devices = lax.axis_size(("el", "tg"))
    groups = lax.axis_size("el")
    packed = pack(owner_map, send_counts, field_points)
    outgoing = packed.reshape(devices, elems // devices * points, channels)
    incoming = lax.all_to_all(outgoing, ("el", "tg"), split_axis=0, concat_axis=0, tiled=True)
    source = incoming.reshape(-1, weights.shape[-1], channels)
    whole = None
    for part in range(PARTS):
        pieces = remap(part, tile_rows, tile_cols, weights, source)
        received = []
        for piece, hop in zip(pieces, HOPS):
            if hop != (0, 0):
                pairs = [(i, (i // 2 + hop[0]) % (groups // 2) * 2 + (i + hop[1]) % 2) for i in range(groups)]
                piece = lax.ppermute(piece, "el", pairs)
            received.append(piece)
        whole = join(part, received, whole)
    return whole


def solution(mesh):
    return jax.shard_map(
        on_device,
        mesh=mesh,
        in_specs=(
            P(("el", "tg"), None, None),
            P(("el", "tg"), None),
            P(("el", "tg"), None),
            P(("el", "tg"), None),
            P(("el", "tg"), None, None),
            P(("el", "tg"), None, None, None, None),
        ),
        out_specs=P("el", "tg"),
        check_vma=False,
    )
```

```python
import functools

import jax
import jax.numpy as jnp
from jax import lax
from jax.experimental import pallas as pl
from jax.experimental.pallas import tpu as pltpu
from jax.sharding import PartitionSpec as P

SHARES = (5, 3)
GROUP = 4
AHEAD = 2
HOPS = ((2, 0), (2, 1), (1, 0), (3, 0), (1, 1), (3, 1), (0, 1), (0, 0))


def pack_kernel(chunks, owner_ref, counts_ref, field_ref, out_ref, buf, dst, pos_v, pos_s, sem_in, sem_pos, sem_out):
    elems, points, channels = dst.shape
    step = elems // chunks
    owners = elems // 4
    def fetch(c):
        return pltpu.make_async_copy(field_ref.at[pl.ds(c * step, step)], buf.at[pl.ds(c * step, step)], sem_in.at[c])
    for c in range(chunks):
        fetch(c).start()
    owner = owner_ref[...]
    hit = lax.broadcasted_iota(jnp.int32, (owners, elems), 0) == owner
    hit = jnp.where(hit, 1.0, 0.0)
    before = jnp.where(lax.broadcasted_iota(jnp.int32, (elems, elems), 0) < lax.broadcasted_iota(jnp.int32, (elems, elems), 1), 1.0, 0.0)
    earlier = jnp.dot(hit.astype(jnp.bfloat16), before.astype(jnp.bfloat16), preferred_element_type=jnp.float32)
    rank = jnp.sum(hit * earlier, axis=0, keepdims=True)
    pos_v[...] = owner * 4 + rank.astype(jnp.int32)
    cp = pltpu.make_async_copy(pos_v, pos_s, sem_pos)
    cp.start()
    cp.wait()
    point = lax.broadcasted_iota(jnp.int32, (points, channels), 0)
    for c in range(chunks):
        fetch(c).wait()
        def body(e, carry):
            live = point < counts_ref[0, e]
            dst[pos_s[0, e]] = jnp.where(live, buf[e], jnp.zeros((), buf.dtype))
            return carry
        lax.fori_loop(c * step, (c + 1) * step, body, 0, unroll=8)
    out = pltpu.make_async_copy(dst, out_ref, sem_out)
    out.start()
    out.wait()


def pack(owner_map, send_counts, field, chunks=8):
    return pl.pallas_call(
        functools.partial(pack_kernel, chunks),
        out_shape=jax.ShapeDtypeStruct(field.shape, field.dtype),
        in_specs=[pl.BlockSpec(memory_space=pltpu.VMEM), pl.BlockSpec(memory_space=pltpu.SMEM), pl.BlockSpec(memory_space=pl.ANY)],
        out_specs=pl.BlockSpec(memory_space=pl.ANY),
        scratch_shapes=[
            pltpu.VMEM(field.shape, field.dtype),
            pltpu.VMEM(field.shape, field.dtype),
            pltpu.VMEM((1, field.shape[0]), jnp.int32),
            pltpu.SMEM((1, field.shape[0]), jnp.int32),
            pltpu.SemaphoreType.DMA((chunks,)),
            pltpu.SemaphoreType.DMA,
            pltpu.SemaphoreType.DMA,
        ],
        name="pack",
    )(owner_map, send_counts, field)


def peer(me, groups, hop):
    chip, core = me // 2, me % 2
    return lax.rem(chip + hop[0], groups // 2) * 2 + (1 - core if hop[1] else core)


def remap_kernel(first, axis, rows_ref, cols_ref, w_ref, src_ref, *refs):
    outs, (w_buf, src, out, order, sem_src, sem_w) = refs[: len(HOPS)], refs[len(HOPS) :]
    _, targets, blocks, tile, _ = w_ref.shape
    count = w_buf.shape[0]
    groups = len(HOPS)
    rows = out.shape[0] // groups
    load = pltpu.make_async_copy(src_ref, src, sem_src)
    load.start()
    for t in range(targets):
        order[rows_ref[0, t]] = t

    def fetch(q):
        return pltpu.make_async_copy(w_ref.at[0, order[first + q]], w_buf.at[q], sem_w.at[q])

    for q in range(min(count, GROUP * AHEAD)):
        fetch(q).start()
    load.wait()
    for g in range(0, count, GROUP):
        for q in range(g, g + GROUP):
            fetch(q).wait()
        for q in range(g + GROUP * AHEAD, min(count, g + GROUP * AHEAD + GROUP)):
            fetch(q).start()
        for q in range(g, g + GROUP):
            t = order[first + q]
            total = None
            for k in range(0, blocks, 2):
                w = jnp.concatenate([w_buf[q, k], w_buf[q, k + 1]], axis=1)
                x = jnp.concatenate([src[cols_ref[0, t, k]], src[cols_ref[0, t, k + 1]]], axis=0)
                r = jnp.dot(w, x, preferred_element_type=jnp.float32)
                total = r if total is None else total + r
            out[:, q * tile : (q + 1) * tile] = total.T.astype(out.dtype)
    me = lax.axis_index(axis) if axis else 0
    for i, hop in enumerate(HOPS):
        row = pl.multiple_of(peer(me, groups, hop) * rows, rows)
        outs[i][...] = out[pl.ds(row, rows)]


def remap(first, count, tile_rows, tile_cols, weights, source, axis="el"):
    _, targets, blocks, tile, _ = weights.shape
    channels = source.shape[-1]
    piece = jax.ShapeDtypeStruct((channels // len(HOPS), count * tile), source.dtype)
    return pl.pallas_call(
        functools.partial(remap_kernel, first, axis),
        out_shape=[piece] * len(HOPS),
        in_specs=[pl.BlockSpec(memory_space=pltpu.SMEM)] * 2 + [pl.BlockSpec(memory_space=pl.ANY)] * 2,
        out_specs=[pl.BlockSpec(memory_space=pltpu.VMEM)] * len(HOPS),
        scratch_shapes=[
            pltpu.VMEM((count, *weights.shape[2:]), weights.dtype),
            pltpu.VMEM(source.shape, source.dtype),
            pltpu.VMEM((channels, count * tile), source.dtype),
            pltpu.SMEM((targets,), jnp.int32),
            pltpu.SemaphoreType.DMA,
            pltpu.SemaphoreType.DMA((count,)),
        ],
        compiler_params=pltpu.CompilerParams(vmem_limit_bytes=46 << 20),
        cost_estimate=pl.CostEstimate(
            flops=2 * count * blocks * tile * tile * channels,
            bytes_accessed=2 * (weights.size * count // targets + source.size),
            transcendentals=0,
        ),
    )(tile_rows, tile_cols, weights, source)


def join_kernel(start, axis, *refs):
    pieces, (out_ref, sems) = refs[: len(HOPS)], refs[-2:]
    me = lax.axis_index(axis) if axis else 0
    groups = len(HOPS)
    width = pieces[0].shape[1]
    stores = []
    for i, (chip, core) in enumerate(HOPS):
        source = peer(me, groups, ((groups // 2 - chip) % (groups // 2), core))
        lane = pl.multiple_of(source * (out_ref.shape[1] // groups) + start, 128)
        stores.append(pltpu.make_async_copy(pieces[i], out_ref.at[:, pl.ds(lane, width)], sems.at[i]))
        stores[i].start()
    for store in stores:
        store.wait()


def join(start, span, pieces, whole=None, axis="el"):
    rows, width = pieces[0].shape
    groups = len(HOPS)
    kept = [] if whole is None else [whole]
    return pl.pallas_call(
        functools.partial(join_kernel, start, axis),
        out_shape=jax.ShapeDtypeStruct((rows, groups * span), pieces[0].dtype),
        in_specs=[pl.BlockSpec(memory_space=pltpu.VMEM)] * groups + [pl.BlockSpec(memory_space=pl.ANY)] * len(kept),
        out_specs=pl.BlockSpec(memory_space=pl.ANY),
        scratch_shapes=[pltpu.SemaphoreType.DMA((groups,))],
        input_output_aliases={groups: 0} if kept else {},
        compiler_params=pltpu.CompilerParams(vmem_limit_bytes=8 << 20),
        cost_estimate=pl.CostEstimate(flops=0, bytes_accessed=4 * groups * rows * width, transcendentals=0),
    )(*pieces, *kept)


def on_device(field_points, owner_map, send_counts, tile_rows, tile_cols, weights):
    elems, points, channels = field_points.shape
    devices = lax.axis_size(("el", "tg"))
    groups = lax.axis_size("el")
    packed = pack(owner_map, send_counts, field_points)
    outgoing = packed.reshape(devices, elems // devices * points, channels)
    incoming = lax.all_to_all(outgoing, ("el", "tg"), split_axis=0, concat_axis=0, tiled=True)
    source = incoming.reshape(-1, weights.shape[-1], channels)
    targets, tile = weights.shape[1], weights.shape[-1]
    whole, first = None, 0
    for share in SHARES:
        count = targets * share // sum(SHARES)
        pieces = remap(first, count, tile_rows, tile_cols, weights, source)
        received = []
        for piece, hop in zip(pieces, HOPS):
            if hop != (0, 0):
                pairs = [(i, (i // 2 + hop[0]) % (groups // 2) * 2 + (i + hop[1]) % 2) for i in range(groups)]
                piece = lax.ppermute(piece, "el", pairs)
            received.append(piece)
        whole = join(first * tile, targets * tile, received, whole)
        first += count
    return whole


def solution(mesh):
    return jax.shard_map(
        on_device,
        mesh=mesh,
        in_specs=(
            P(("el", "tg"), None, None),
            P(("el", "tg"), None),
            P(("el", "tg"), None),
            P(("el", "tg"), None),
            P(("el", "tg"), None, None),
            P(("el", "tg"), None, None, None, None),
        ),
        out_specs=P("el", "tg"),
        check_vma=False,
    )
```

```python
import functools

import jax
import jax.numpy as jnp
from jax import lax
from jax.experimental import pallas as pl
from jax.experimental.pallas import tpu as pltpu
from jax.sharding import PartitionSpec as P

SHARES = (1, 1)
CHIPS = (2, 1, 3, 0)
GROUP = 4
AHEAD = 2
HOPS = ((2, 0), (2, 1), (1, 0), (3, 0), (1, 1), (3, 1), (0, 1), (0, 0))


def pack_kernel(chunks, owner_ref, counts_ref, field_ref, out_ref, buf, dst, pos_v, pos_s, sem_in, sem_pos, sem_out):
    elems, points, channels = dst.shape
    step = elems // chunks
    owners = elems // 4
    def fetch(c):
        return pltpu.make_async_copy(field_ref.at[pl.ds(c * step, step)], buf.at[pl.ds(c * step, step)], sem_in.at[c])
    for c in range(chunks):
        fetch(c).start()
    owner = owner_ref[...]
    hit = lax.broadcasted_iota(jnp.int32, (owners, elems), 0) == owner
    hit = jnp.where(hit, 1.0, 0.0)
    before = jnp.where(lax.broadcasted_iota(jnp.int32, (elems, elems), 0) < lax.broadcasted_iota(jnp.int32, (elems, elems), 1), 1.0, 0.0)
    earlier = jnp.dot(hit.astype(jnp.bfloat16), before.astype(jnp.bfloat16), preferred_element_type=jnp.float32)
    rank = jnp.sum(hit * earlier, axis=0, keepdims=True)
    pos_v[...] = owner * 4 + rank.astype(jnp.int32)
    cp = pltpu.make_async_copy(pos_v, pos_s, sem_pos)
    cp.start()
    cp.wait()
    point = lax.broadcasted_iota(jnp.int32, (points, channels), 0)
    for c in range(chunks):
        fetch(c).wait()
        def body(e, carry):
            live = point < counts_ref[0, e]
            dst[pos_s[0, e]] = jnp.where(live, buf[e], jnp.zeros((), buf.dtype))
            return carry
        lax.fori_loop(c * step, (c + 1) * step, body, 0, unroll=8)
    out = pltpu.make_async_copy(dst, out_ref, sem_out)
    out.start()
    out.wait()


def pack(owner_map, send_counts, field, chunks=8):
    return pl.pallas_call(
        functools.partial(pack_kernel, chunks),
        out_shape=jax.ShapeDtypeStruct(field.shape, field.dtype),
        in_specs=[pl.BlockSpec(memory_space=pltpu.VMEM), pl.BlockSpec(memory_space=pltpu.SMEM), pl.BlockSpec(memory_space=pl.ANY)],
        out_specs=pl.BlockSpec(memory_space=pl.ANY),
        scratch_shapes=[
            pltpu.VMEM(field.shape, field.dtype),
            pltpu.VMEM(field.shape, field.dtype),
            pltpu.VMEM((1, field.shape[0]), jnp.int32),
            pltpu.SMEM((1, field.shape[0]), jnp.int32),
            pltpu.SemaphoreType.DMA((chunks,)),
            pltpu.SemaphoreType.DMA,
            pltpu.SemaphoreType.DMA,
        ],
        name="pack",
    )(owner_map, send_counts, field)


HOPS_OF = {False: HOPS, True: tuple((chip, 0) for chip in CHIPS)}


def peer(me, groups, hop):
    chip, core = me // 2, me % 2
    return lax.rem(chip + hop[0], groups // 2) * 2 + (1 - core if hop[1] else core)


def remap_kernel(first, paired, axis, rows_ref, cols_ref, w_ref, src_ref, *refs):
    outs, (w_buf, src, out, order, sem_src, sem_w) = refs[:-6], refs[-6:]
    _, targets, blocks, tile, _ = w_ref.shape
    count = w_buf.shape[0]
    groups = len(HOPS)
    rows = out.shape[0] // groups
    load = pltpu.make_async_copy(src_ref, src, sem_src)
    load.start()
    for t in range(targets):
        order[rows_ref[0, t]] = t

    def fetch(q):
        return pltpu.make_async_copy(w_ref.at[0, order[first + q]], w_buf.at[q], sem_w.at[q])

    for q in range(min(count, GROUP * AHEAD)):
        fetch(q).start()
    load.wait()
    for g in range(0, count, GROUP):
        for q in range(g, g + GROUP):
            fetch(q).wait()
        for q in range(g + GROUP * AHEAD, min(count, g + GROUP * AHEAD + GROUP)):
            fetch(q).start()
        for q in range(g, g + GROUP):
            t = order[first + q]
            total = None
            for k in range(0, blocks, 2):
                w = jnp.concatenate([w_buf[q, k], w_buf[q, k + 1]], axis=1)
                x = jnp.concatenate([src[cols_ref[0, t, k]], src[cols_ref[0, t, k + 1]]], axis=0)
                r = jnp.dot(w, x, preferred_element_type=jnp.float32)
                total = r if total is None else total + r
            out[:, q * tile : (q + 1) * tile] = total.T.astype(out.dtype)
    me = lax.axis_index(axis) if axis else 0
    for piece, hop in zip(outs, HOPS_OF[paired]):
        row = peer(me, groups, hop) // 2 * 2 if paired else peer(me, groups, hop)
        piece[...] = out[pl.ds(pl.multiple_of(row * rows, rows), piece.shape[0])]


def remap(first, count, paired, tile_rows, tile_cols, weights, source, axis="el"):
    _, targets, blocks, tile, _ = weights.shape
    channels = source.shape[-1]
    pieces = len(HOPS_OF[paired])
    piece = jax.ShapeDtypeStruct((channels // pieces, count * tile), source.dtype)
    return pl.pallas_call(
        functools.partial(remap_kernel, first, paired, axis),
        out_shape=[piece] * pieces,
        in_specs=[pl.BlockSpec(memory_space=pltpu.SMEM)] * 2 + [pl.BlockSpec(memory_space=pl.ANY)] * 2,
        out_specs=[pl.BlockSpec(memory_space=pltpu.VMEM)] * pieces,
        scratch_shapes=[
            pltpu.VMEM((count, *weights.shape[2:]), weights.dtype),
            pltpu.VMEM(source.shape, source.dtype),
            pltpu.VMEM((channels, count * tile), source.dtype),
            pltpu.SMEM((targets,), jnp.int32),
            pltpu.SemaphoreType.DMA,
            pltpu.SemaphoreType.DMA((count,)),
        ],
        compiler_params=pltpu.CompilerParams(vmem_limit_bytes=46 << 20),
        cost_estimate=pl.CostEstimate(
            flops=2 * count * blocks * tile * tile * channels,
            bytes_accessed=2 * (weights.size * count // targets + source.size),
            transcendentals=0,
        ),
    )(tile_rows, tile_cols, weights, source)


def place(me, groups, start, piece, hop, out_ref, sem):
    chip, core = hop
    source = peer(me, groups, ((groups // 2 - chip) % (groups // 2), core))
    lane = pl.multiple_of(source * (out_ref.shape[1] // groups) + start, 128)
    return pltpu.make_async_copy(piece, out_ref.at[:, pl.ds(lane, piece.shape[1])], sem)


def join_kernel(start, groups, hops, axis, *refs):
    out_ref, sems = refs[-2:]
    me = lax.axis_index(axis) if axis else 0
    rows = out_ref.shape[0]
    stores = []
    for i, hop in enumerate(hops):
        piece = refs[i] if len(hops) == groups else refs[0].at[pl.ds(i * rows, rows)]
        stores.append(place(me, groups, start, piece, hop, out_ref, sems.at[i]))
        stores[i].start()
    for store in stores:
        store.wait()


def join(start, hops, groups, pieces, whole, axis="el"):
    return pl.pallas_call(
        functools.partial(join_kernel, start, groups, hops, axis),
        out_shape=jax.ShapeDtypeStruct(whole.shape, whole.dtype),
        in_specs=[pl.BlockSpec(memory_space=pltpu.VMEM)] * len(pieces) + [pl.BlockSpec(memory_space=pl.ANY)],
        out_specs=pl.BlockSpec(memory_space=pl.ANY),
        scratch_shapes=[pltpu.SemaphoreType.DMA((len(hops),))],
        input_output_aliases={len(pieces): 0},
        compiler_params=pltpu.CompilerParams(vmem_limit_bytes=8 << 20),
        cost_estimate=pl.CostEstimate(flops=0, bytes_accessed=4 * sum(p.size for p in pieces), transcendentals=0),
    )(*pieces, whole)


def split_kernel(start, groups, axis, *refs):
    pieces, (out_ref, away_ref, sems) = refs[: len(CHIPS)], refs[-3:]
    me = lax.axis_index(axis) if axis else 0
    core = me % 2
    rows = out_ref.shape[0]
    stores = []
    for i, chip in enumerate(CHIPS):
        kept = pieces[i].at[pl.ds(pl.multiple_of(core * rows, rows), rows)]
        stores.append(place(me, groups, start, kept, (chip, 0), out_ref, sems.at[i]))
        stores[i].start()
    for i in range(len(CHIPS)):
        away_ref[i * rows : (i + 1) * rows] = pieces[i][pl.ds(pl.multiple_of((1 - core) * rows, rows), rows)]
    for store in stores:
        store.wait()


def split(start, span, groups, pieces, axis="el"):
    rows, width = pieces[0].shape[0] // 2, pieces[0].shape[1]
    dtype = pieces[0].dtype
    return pl.pallas_call(
        functools.partial(split_kernel, start, groups, axis),
        out_shape=[
            jax.ShapeDtypeStruct((rows, groups * span), dtype),
            jax.ShapeDtypeStruct((len(CHIPS) * rows, width), dtype),
        ],
        in_specs=[pl.BlockSpec(memory_space=pltpu.VMEM)] * len(pieces),
        out_specs=[pl.BlockSpec(memory_space=pl.ANY), pl.BlockSpec(memory_space=pltpu.VMEM)],
        scratch_shapes=[pltpu.SemaphoreType.DMA((len(CHIPS),))],
        compiler_params=pltpu.CompilerParams(vmem_limit_bytes=8 << 20),
        cost_estimate=pl.CostEstimate(flops=0, bytes_accessed=4 * sum(p.size for p in pieces), transcendentals=0),
    )(*pieces)


def send(piece, groups, hop):
    if hop == (0, 0):
        return piece
    pairs = [(i, (i // 2 + hop[0]) % (groups // 2) * 2 + (i + hop[1]) % 2) for i in range(groups)]
    return lax.ppermute(piece, "el", pairs)


def on_device(field_points, owner_map, send_counts, tile_rows, tile_cols, weights):
    elems, points, channels = field_points.shape
    devices = lax.axis_size(("el", "tg"))
    groups = lax.axis_size("el")
    packed = pack(owner_map, send_counts, field_points)
    outgoing = packed.reshape(devices, elems // devices * points, channels)
    incoming = lax.all_to_all(outgoing, ("el", "tg"), split_axis=0, concat_axis=0, tiled=True)
    source = incoming.reshape(-1, weights.shape[-1], channels)
    targets, tile = weights.shape[1], weights.shape[-1]
    count = targets * SHARES[0] // sum(SHARES)
    pieces = remap(0, count, True, tile_rows, tile_cols, weights, source)
    received = [send(piece, groups, hop) for piece, hop in zip(pieces, HOPS_OF[True])]
    pieces = remap(count, targets - count, False, tile_rows, tile_cols, weights, source)
    whole, away = split(0, targets * tile, groups, received)
    away = send(away, groups, (0, 1))
    received = [send(piece, groups, hop) for piece, hop in zip(pieces, HOPS)]
    whole = join(0, tuple((chip, 1) for chip in CHIPS), groups, [away], whole)
    whole = join(count * tile, HOPS, groups, received, whole)
    return whole


def solution(mesh):
    return jax.shard_map(
        on_device,
        mesh=mesh,
        in_specs=(
            P(("el", "tg"), None, None),
            P(("el", "tg"), None),
            P(("el", "tg"), None),
            P(("el", "tg"), None),
            P(("el", "tg"), None, None),
            P(("el", "tg"), None, None, None, None),
        ),
        out_specs=P("el", "tg"),
        check_vma=False,
    )
```

```python
import functools

import jax
import jax.numpy as jnp
from jax import lax
from jax.experimental import pallas as pl
from jax.experimental.pallas import tpu as pltpu
from jax.sharding import PartitionSpec as P

SHARES = (7, 9)
STAGED = 6
CHIPS = (2, 1, 3, 0)
GROUP = 4
AHEAD = 2
HOPS = ((2, 0), (2, 1), (1, 0), (3, 0), (1, 1), (3, 1), (0, 1), (0, 0))


def pack_kernel(chunks, owner_ref, counts_ref, field_ref, out_ref, buf, dst, pos_v, pos_s, sem_in, sem_pos, sem_out):
    elems, points, channels = dst.shape
    step = elems // chunks
    owners = elems // 4
    def fetch(c):
        return pltpu.make_async_copy(field_ref.at[pl.ds(c * step, step)], buf.at[pl.ds(c * step, step)], sem_in.at[c])
    for c in range(chunks):
        fetch(c).start()
    owner = owner_ref[...]
    hit = lax.broadcasted_iota(jnp.int32, (owners, elems), 0) == owner
    hit = jnp.where(hit, 1.0, 0.0)
    before = jnp.where(lax.broadcasted_iota(jnp.int32, (elems, elems), 0) < lax.broadcasted_iota(jnp.int32, (elems, elems), 1), 1.0, 0.0)
    earlier = jnp.dot(hit.astype(jnp.bfloat16), before.astype(jnp.bfloat16), preferred_element_type=jnp.float32)
    rank = jnp.sum(hit * earlier, axis=0, keepdims=True)
    pos_v[...] = owner * 4 + rank.astype(jnp.int32)
    cp = pltpu.make_async_copy(pos_v, pos_s, sem_pos)
    cp.start()
    cp.wait()
    point = lax.broadcasted_iota(jnp.int32, (points, channels), 0)
    for c in range(chunks):
        fetch(c).wait()
        def body(e, carry):
            live = point < counts_ref[0, e]
            dst[pos_s[0, e]] = jnp.where(live, buf[e], jnp.zeros((), buf.dtype))
            return carry
        lax.fori_loop(c * step, (c + 1) * step, body, 0, unroll=8)
    out = pltpu.make_async_copy(dst, out_ref, sem_out)
    out.start()
    out.wait()


def pack(owner_map, send_counts, field, chunks=8):
    return pl.pallas_call(
        functools.partial(pack_kernel, chunks),
        out_shape=jax.ShapeDtypeStruct(field.shape, field.dtype),
        in_specs=[pl.BlockSpec(memory_space=pltpu.VMEM), pl.BlockSpec(memory_space=pltpu.SMEM), pl.BlockSpec(memory_space=pl.ANY)],
        out_specs=pl.BlockSpec(memory_space=pl.ANY),
        scratch_shapes=[
            pltpu.VMEM(field.shape, field.dtype),
            pltpu.VMEM(field.shape, field.dtype),
            pltpu.VMEM((1, field.shape[0]), jnp.int32),
            pltpu.SMEM((1, field.shape[0]), jnp.int32),
            pltpu.SemaphoreType.DMA((chunks,)),
            pltpu.SemaphoreType.DMA,
            pltpu.SemaphoreType.DMA,
        ],
        name="pack",
    )(owner_map, send_counts, field)


HOPS_OF = {False: HOPS, True: tuple((chip, 0) for chip in CHIPS)}


def peer(me, groups, hop):
    chip, core = me // 2, me % 2
    return lax.rem(chip + hop[0], groups // 2) * 2 + (1 - core if hop[1] else core)


def stage_kernel(rows_ref, w_ref, out_ref, order, sems):
    for t in range(rows_ref.shape[1]):
        order[rows_ref[0, t]] = t
    copies = [pltpu.make_async_copy(w_ref.at[0, order[q]], out_ref.at[q], sems.at[q]) for q in range(STAGED)]
    for copy in copies:
        copy.start()
    for copy in copies:
        copy.wait()


def stage(tile_rows, weights):
    return pl.pallas_call(
        stage_kernel,
        out_shape=jax.ShapeDtypeStruct((STAGED, *weights.shape[2:]), weights.dtype),
        in_specs=[pl.BlockSpec(memory_space=pltpu.SMEM), pl.BlockSpec(memory_space=pl.ANY)],
        out_specs=pl.BlockSpec(memory_space=pltpu.VMEM),
        scratch_shapes=[pltpu.SMEM(tile_rows.shape[1:], jnp.int32), pltpu.SemaphoreType.DMA((STAGED,))],
        compiler_params=pltpu.CompilerParams(vmem_limit_bytes=46 << 20),
        cost_estimate=pl.CostEstimate(flops=0, bytes_accessed=4 * STAGED * weights[0, 0].size, transcendentals=0),
        name="stage",
    )(tile_rows, weights)


def remap_kernel(first, staged, paired, axis, rows_ref, cols_ref, w_ref, src_ref, *refs):
    outs, (w_buf, out, order, sem_src, sem_w) = list(refs[staged > 0 : -5]), refs[-5:]
    src = src_ref
    _, targets, blocks, tile, _ = w_ref.shape
    count = out.shape[1] // tile
    groups = len(HOPS)
    rows = out.shape[0] // groups
    if staged:
        src = outs.pop()
        load = pltpu.make_async_copy(src_ref, src, sem_src)
        load.start()
    for t in range(targets):
        order[rows_ref[0, t]] = t

    def fetch(q):
        return pltpu.make_async_copy(w_ref.at[0, order[first + q]], w_buf.at[q - staged], sem_w.at[q - staged])

    def block(q, k):
        return refs[0][q, k] if q < staged else w_buf[q - staged, k]

    for q in range(staged, GROUP * AHEAD):
        fetch(q).start()
    if staged:
        load.wait()
    for g in range(0, count, GROUP):
        for q in range(max(g, staged), min(count, g + GROUP)):
            fetch(q).wait()
        for q in range(g + GROUP * AHEAD, min(count, g + GROUP * AHEAD + GROUP)):
            fetch(q).start()
        for q in range(g, min(count, g + GROUP)):
            t = order[first + q]
            total = None
            for k in range(0, blocks, 2):
                w = jnp.concatenate([block(q, k), block(q, k + 1)], axis=1)
                x = jnp.concatenate([src[cols_ref[0, t, k]], src[cols_ref[0, t, k + 1]]], axis=0)
                r = jnp.dot(w, x, preferred_element_type=jnp.float32)
                total = r if total is None else total + r
            out[:, q * tile : (q + 1) * tile] = total.T.astype(out.dtype)
    me = lax.axis_index(axis) if axis else 0
    for piece, hop in zip(outs, HOPS_OF[paired]):
        row = peer(me, groups, hop) // 2 * 2 if paired else peer(me, groups, hop)
        piece[...] = out[pl.ds(pl.multiple_of(row * rows, rows), piece.shape[0])]


def remap(first, count, paired, tile_rows, tile_cols, weights, source, ready=None, axis="el"):
    _, targets, blocks, tile, _ = weights.shape
    channels = source.shape[-1]
    staged = 0 if ready is None else STAGED
    pieces = len(HOPS_OF[paired])
    shapes = [jax.ShapeDtypeStruct((channels // pieces, count * tile), source.dtype)] * pieces
    vmem = pl.BlockSpec(memory_space=pltpu.VMEM)
    held = [pl.BlockSpec(memory_space=pl.ANY), vmem] if staged else [vmem]
    if staged:
        shapes.append(jax.ShapeDtypeStruct(source.shape, source.dtype))
    return pl.pallas_call(
        functools.partial(remap_kernel, first, staged, paired, axis),
        out_shape=shapes,
        in_specs=[pl.BlockSpec(memory_space=pltpu.SMEM)] * 2 + [pl.BlockSpec(memory_space=pl.ANY)] + held,
        out_specs=[vmem] * len(shapes),
        scratch_shapes=[
            pltpu.VMEM((count - staged, *weights.shape[2:]), weights.dtype),
            pltpu.VMEM((channels, count * tile), source.dtype),
            pltpu.SMEM((targets,), jnp.int32),
            pltpu.SemaphoreType.DMA,
            pltpu.SemaphoreType.DMA((count - staged,)),
        ],
        compiler_params=pltpu.CompilerParams(vmem_limit_bytes=46 << 20),
        cost_estimate=pl.CostEstimate(
            flops=2 * count * blocks * tile * tile * channels,
            bytes_accessed=2 * (weights.size * count // targets + source.size),
            transcendentals=0,
        ),
    )(tile_rows, tile_cols, weights, source, *([ready] if staged else []))


def place(me, groups, start, piece, hop, out_ref, sem):
    chip, core = hop
    source = peer(me, groups, ((groups // 2 - chip) % (groups // 2), core))
    lane = pl.multiple_of(source * (out_ref.shape[1] // groups) + start, 128)
    return pltpu.make_async_copy(piece, out_ref.at[:, pl.ds(lane, piece.shape[1])], sem)


def join_kernel(start, groups, hops, axis, *refs):
    out_ref, sems = refs[-2:]
    me = lax.axis_index(axis) if axis else 0
    rows = out_ref.shape[0]
    stores = []
    for i, hop in enumerate(hops):
        piece = refs[i] if len(hops) == groups else refs[0].at[pl.ds(i * rows, rows)]
        stores.append(place(me, groups, start, piece, hop, out_ref, sems.at[i]))
        stores[i].start()
    for store in stores:
        store.wait()


def join(start, hops, groups, pieces, whole, axis="el"):
    return pl.pallas_call(
        functools.partial(join_kernel, start, groups, hops, axis),
        out_shape=jax.ShapeDtypeStruct(whole.shape, whole.dtype),
        in_specs=[pl.BlockSpec(memory_space=pltpu.VMEM)] * len(pieces) + [pl.BlockSpec(memory_space=pl.ANY)],
        out_specs=pl.BlockSpec(memory_space=pl.ANY),
        scratch_shapes=[pltpu.SemaphoreType.DMA((len(hops),))],
        input_output_aliases={len(pieces): 0},
        compiler_params=pltpu.CompilerParams(vmem_limit_bytes=8 << 20),
        cost_estimate=pl.CostEstimate(flops=0, bytes_accessed=4 * sum(p.size for p in pieces), transcendentals=0),
    )(*pieces, whole)


def split_kernel(start, groups, axis, *refs):
    pieces, (out_ref, away_ref, sems) = refs[: len(CHIPS)], refs[-3:]
    me = lax.axis_index(axis) if axis else 0
    core = me % 2
    rows = out_ref.shape[0]
    stores = []
    for i, chip in enumerate(CHIPS):
        kept = pieces[i].at[pl.ds(pl.multiple_of(core * rows, rows), rows)]
        stores.append(place(me, groups, start, kept, (chip, 0), out_ref, sems.at[i]))
        stores[i].start()
    for i in range(len(CHIPS)):
        away_ref[i * rows : (i + 1) * rows] = pieces[i][pl.ds(pl.multiple_of((1 - core) * rows, rows), rows)]
    for store in stores:
        store.wait()


def split(start, span, groups, pieces, axis="el"):
    rows, width = pieces[0].shape[0] // 2, pieces[0].shape[1]
    dtype = pieces[0].dtype
    return pl.pallas_call(
        functools.partial(split_kernel, start, groups, axis),
        out_shape=[
            jax.ShapeDtypeStruct((rows, groups * span), dtype),
            jax.ShapeDtypeStruct((len(CHIPS) * rows, width), dtype),
        ],
        in_specs=[pl.BlockSpec(memory_space=pltpu.VMEM)] * len(pieces),
        out_specs=[pl.BlockSpec(memory_space=pl.ANY), pl.BlockSpec(memory_space=pltpu.VMEM)],
        scratch_shapes=[pltpu.SemaphoreType.DMA((len(CHIPS),))],
        compiler_params=pltpu.CompilerParams(vmem_limit_bytes=8 << 20),
        cost_estimate=pl.CostEstimate(flops=0, bytes_accessed=4 * sum(p.size for p in pieces), transcendentals=0),
    )(*pieces)


def send(piece, groups, hop):
    if hop == (0, 0):
        return piece
    pairs = [(i, (i // 2 + hop[0]) % (groups // 2) * 2 + (i + hop[1]) % 2) for i in range(groups)]
    return lax.ppermute(piece, "el", pairs)


def on_device(field_points, owner_map, send_counts, tile_rows, tile_cols, weights):
    elems, points, channels = field_points.shape
    devices = lax.axis_size(("el", "tg"))
    groups = lax.axis_size("el")
    packed = pack(owner_map, send_counts, field_points)
    outgoing = packed.reshape(devices, elems // devices * points, channels)
    incoming = lax.all_to_all(outgoing, ("el", "tg"), split_axis=0, concat_axis=0, tiled=True)
    ready = stage(tile_rows, weights)
    source = incoming.reshape(-1, weights.shape[-1], channels)
    targets, tile = weights.shape[1], weights.shape[-1]
    count = targets * SHARES[0] // sum(SHARES)
    *pieces, source = remap(0, count, True, tile_rows, tile_cols, weights, source, ready)
    received = [send(piece, groups, hop) for piece, hop in zip(pieces, HOPS_OF[True])]
    pieces = remap(count, targets - count, False, tile_rows, tile_cols, weights, source)
    whole, away = split(0, targets * tile, groups, received)
    away = send(away, groups, (0, 1))
    received = [send(piece, groups, hop) for piece, hop in zip(pieces, HOPS)]
    whole = join(0, tuple((chip, 1) for chip in CHIPS), groups, [away], whole)
    whole = join(count * tile, HOPS, groups, received, whole)
    return whole


def solution(mesh):
    return jax.shard_map(
        on_device,
        mesh=mesh,
        in_specs=(
            P(("el", "tg"), None, None),
            P(("el", "tg"), None),
            P(("el", "tg"), None),
            P(("el", "tg"), None),
            P(("el", "tg"), None, None),
            P(("el", "tg"), None, None, None, None),
        ),
        out_specs=P("el", "tg"),
        check_vma=False,
    )
```

```python
import functools

import jax
import jax.numpy as jnp
from jax import lax
from jax.experimental import pallas as pl
from jax.experimental.pallas import tpu as pltpu
from jax.sharding import PartitionSpec as P

SHARES = (7, 9)
STAGED = 6
CHIPS = (1, 3, 2, 0)
EARLY = (0, 1, 2, 3, 6, 7)
LATE = (4, 5)
GROUP = 4
AHEAD = 2
HOPS = ((2, 0), (2, 1), (1, 0), (3, 0), (1, 1), (3, 1), (0, 1), (0, 0))


def pack_kernel(chunks, owner_ref, counts_ref, field_ref, out_ref, buf, dst, pos_v, pos_s, sem_in, sem_pos, sem_out):
    elems, points, channels = dst.shape
    step = elems // chunks
    owners = elems // 4

    def fetch(c):
        return pltpu.make_async_copy(field_ref.at[pl.ds(c * step, step)], buf.at[pl.ds(c * step, step)], sem_in.at[c])

    for c in range(chunks):
        fetch(c).start()
    owner = owner_ref[...]
    hit = lax.broadcasted_iota(jnp.int32, (owners, elems), 0) == owner
    hit = jnp.where(hit, 1.0, 0.0)
    before = jnp.where(lax.broadcasted_iota(jnp.int32, (elems, elems), 0) < lax.broadcasted_iota(jnp.int32, (elems, elems), 1), 1.0, 0.0)
    earlier = jnp.dot(hit.astype(jnp.bfloat16), before.astype(jnp.bfloat16), preferred_element_type=jnp.float32)
    rank = jnp.sum(hit * earlier, axis=0, keepdims=True)
    pos_v[...] = owner * 4 + rank.astype(jnp.int32)
    cp = pltpu.make_async_copy(pos_v, pos_s, sem_pos)
    cp.start()
    cp.wait()
    point = lax.broadcasted_iota(jnp.int32, (points, channels), 0)
    for c in range(chunks):
        fetch(c).wait()

        def body(e, carry):
            live = point < counts_ref[0, e]
            dst[pos_s[0, e]] = jnp.where(live, buf[e], jnp.zeros((), buf.dtype))
            return carry

        lax.fori_loop(c * step, (c + 1) * step, body, 0, unroll=8)
    out = pltpu.make_async_copy(dst, out_ref, sem_out)
    out.start()
    out.wait()


def pack(owner_map, send_counts, field, chunks=8):
    return pl.pallas_call(
        functools.partial(pack_kernel, chunks),
        out_shape=jax.ShapeDtypeStruct(field.shape, field.dtype),
        in_specs=[pl.BlockSpec(memory_space=pltpu.VMEM), pl.BlockSpec(memory_space=pltpu.SMEM), pl.BlockSpec(memory_space=pl.ANY)],
        out_specs=pl.BlockSpec(memory_space=pl.ANY),
        scratch_shapes=[
            pltpu.VMEM(field.shape, field.dtype),
            pltpu.VMEM(field.shape, field.dtype),
            pltpu.VMEM((1, field.shape[0]), jnp.int32),
            pltpu.SMEM((1, field.shape[0]), jnp.int32),
            pltpu.SemaphoreType.DMA((chunks,)),
            pltpu.SemaphoreType.DMA,
            pltpu.SemaphoreType.DMA,
        ],
        name="pack",
    )(owner_map, send_counts, field)


HOPS_OF = {False: HOPS, True: tuple((chip, 0) for chip in CHIPS)}


def peer(me, groups, hop):
    chip, core = me // 2, me % 2
    return lax.rem(chip + hop[0], groups // 2) * 2 + (1 - core if hop[1] else core)


def stage_kernel(rows_ref, w_ref, out_ref, order, sems):
    for t in range(rows_ref.shape[1]):
        order[rows_ref[0, t]] = t
    copies = [pltpu.make_async_copy(w_ref.at[0, order[q]], out_ref.at[q], sems.at[q]) for q in range(STAGED)]
    for copy in copies:
        copy.start()
    for copy in copies:
        copy.wait()


def stage(tile_rows, weights):
    return pl.pallas_call(
        stage_kernel,
        out_shape=jax.ShapeDtypeStruct((STAGED, *weights.shape[2:]), weights.dtype),
        in_specs=[pl.BlockSpec(memory_space=pltpu.SMEM), pl.BlockSpec(memory_space=pl.ANY)],
        out_specs=pl.BlockSpec(memory_space=pltpu.VMEM),
        scratch_shapes=[pltpu.SMEM(tile_rows.shape[1:], jnp.int32), pltpu.SemaphoreType.DMA((STAGED,))],
        compiler_params=pltpu.CompilerParams(vmem_limit_bytes=46 << 20),
        cost_estimate=pl.CostEstimate(flops=0, bytes_accessed=4 * STAGED * weights[0, 0].size, transcendentals=0),
        name="stage",
    )(tile_rows, weights)


def remap_kernel(first, staged, paired, axis, rows_ref, cols_ref, w_ref, src_ref, *refs):
    outs, (w_buf, out, order, sem_src, sem_w) = list(refs[staged > 0 : -5]), refs[-5:]
    src = src_ref
    _, targets, blocks, tile, _ = w_ref.shape
    count = out.shape[1] // tile
    groups = len(HOPS)
    rows = out.shape[0] // groups
    if staged:
        src = outs.pop()
        load = pltpu.make_async_copy(src_ref, src, sem_src)
        load.start()
    for t in range(targets):
        order[rows_ref[0, t]] = t

    def fetch(q):
        return pltpu.make_async_copy(w_ref.at[0, order[first + q]], w_buf.at[q - staged], sem_w.at[q - staged])

    def block(q, k):
        return refs[0][q, k] if q < staged else w_buf[q - staged, k]

    for q in range(staged, GROUP * AHEAD):
        fetch(q).start()
    me = lax.axis_index(axis) if axis else 0
    places = [peer(me, groups, hop) // 2 * 2 if paired else peer(me, groups, hop) for hop in HOPS_OF[paired]]

    def hand_out(g):
        lanes = slice(g * tile, min(count, g + GROUP) * tile)
        for piece, row in zip(outs, places):
            piece[:, lanes] = out[pl.ds(pl.multiple_of(row * rows, rows), piece.shape[0]), lanes]

    ahead = GROUP * AHEAD
    if staged:
        load.wait()
        for q in range(ahead, ahead + GROUP):
            fetch(q).start()
        ahead += GROUP
    for g in range(0, count, GROUP):
        for q in range(max(g, staged), min(count, g + GROUP)):
            fetch(q).wait()
        for q in range(g + ahead, min(count, g + ahead + GROUP)):
            fetch(q).start()
        if g:
            hand_out(g - GROUP)
        for q in range(g, min(count, g + GROUP)):
            t = order[first + q]
            total = None
            for k in range(0, blocks, 2):
                w = jnp.concatenate([block(q, k), block(q, k + 1)], axis=1)
                x = jnp.concatenate([src[cols_ref[0, t, k]], src[cols_ref[0, t, k + 1]]], axis=0)
                r = jnp.dot(w, x, preferred_element_type=jnp.float32)
                total = r if total is None else total + r
            out[:, q * tile : (q + 1) * tile] = total.T.astype(out.dtype)
    hand_out(count - 1 - (count - 1) % GROUP)


def remap(first, count, paired, tile_rows, tile_cols, weights, source, ready=None, axis="el"):
    _, targets, blocks, tile, _ = weights.shape
    channels = source.shape[-1]
    staged = 0 if ready is None else STAGED
    pieces = len(HOPS_OF[paired])
    shapes = [jax.ShapeDtypeStruct((channels // pieces, count * tile), source.dtype)] * pieces
    vmem = pl.BlockSpec(memory_space=pltpu.VMEM)
    held = [pl.BlockSpec(memory_space=pl.ANY), vmem] if staged else [vmem]
    if staged:
        shapes.append(jax.ShapeDtypeStruct(source.shape, source.dtype))
    return pl.pallas_call(
        functools.partial(remap_kernel, first, staged, paired, axis),
        out_shape=shapes,
        in_specs=[pl.BlockSpec(memory_space=pltpu.SMEM)] * 2 + [pl.BlockSpec(memory_space=pl.ANY)] + held,
        out_specs=[vmem] * len(shapes),
        scratch_shapes=[
            pltpu.VMEM((count - staged, *weights.shape[2:]), weights.dtype),
            pltpu.VMEM((channels, count * tile), source.dtype),
            pltpu.SMEM((targets,), jnp.int32),
            pltpu.SemaphoreType.DMA,
            pltpu.SemaphoreType.DMA((count - staged,)),
        ],
        compiler_params=pltpu.CompilerParams(vmem_limit_bytes=46 << 20),
        cost_estimate=pl.CostEstimate(
            flops=2 * count * blocks * tile * tile * channels,
            bytes_accessed=2 * (weights.size * count // targets + source.size),
            transcendentals=0,
        ),
    )(tile_rows, tile_cols, weights, source, *([ready] if staged else []))


def place(me, groups, start, piece, hop, out_ref, sem):
    chip, core = hop
    source = peer(me, groups, ((groups // 2 - chip) % (groups // 2), core))
    lane = pl.multiple_of(source * (out_ref.shape[1] // groups) + start, 128)
    return pltpu.make_async_copy(piece, out_ref.at[:, pl.ds(lane, piece.shape[1])], sem)


def join_kernel(start, groups, hops, axis, *refs):
    out_ref, sems = refs[-2:]
    me = lax.axis_index(axis) if axis else 0
    rows = out_ref.shape[0]
    stores = []
    for i, hop in enumerate(hops):
        piece = refs[i] if len(refs) > 4 else refs[0].at[pl.ds(i * rows, rows)]
        stores.append(place(me, groups, start, piece, hop, out_ref, sems.at[i]))
        stores[i].start()
    for store in stores:
        store.wait()


def join(start, hops, groups, pieces, whole, axis="el"):
    return pl.pallas_call(
        functools.partial(join_kernel, start, groups, hops, axis),
        out_shape=jax.ShapeDtypeStruct(whole.shape, whole.dtype),
        in_specs=[pl.BlockSpec(memory_space=pltpu.VMEM)] * len(pieces) + [pl.BlockSpec(memory_space=pl.ANY)],
        out_specs=pl.BlockSpec(memory_space=pl.ANY),
        scratch_shapes=[pltpu.SemaphoreType.DMA((len(hops),))],
        input_output_aliases={len(pieces): 0},
        compiler_params=pltpu.CompilerParams(vmem_limit_bytes=8 << 20),
        cost_estimate=pl.CostEstimate(flops=0, bytes_accessed=4 * sum(p.size for p in pieces), transcendentals=0),
    )(*pieces, whole)


def split_kernel(start, groups, axis, *refs):
    pieces, (out_ref, away_ref, sems) = refs[: len(CHIPS)], refs[-3:]
    me = lax.axis_index(axis) if axis else 0
    core = me % 2
    rows = out_ref.shape[0]
    stores = []
    for i, chip in enumerate(CHIPS):
        kept = pieces[i].at[pl.ds(pl.multiple_of(core * rows, rows), rows)]
        stores.append(place(me, groups, start, kept, (chip, 0), out_ref, sems.at[i]))
        stores[i].start()
    for i in range(len(CHIPS)):
        away_ref[i * rows : (i + 1) * rows] = pieces[i][pl.ds(pl.multiple_of((1 - core) * rows, rows), rows)]
    for store in stores:
        store.wait()


def split(start, span, groups, pieces, axis="el"):
    rows, width = pieces[0].shape[0] // 2, pieces[0].shape[1]
    dtype = pieces[0].dtype
    return pl.pallas_call(
        functools.partial(split_kernel, start, groups, axis),
        out_shape=[
            jax.ShapeDtypeStruct((rows, groups * span), dtype),
            jax.ShapeDtypeStruct((len(CHIPS) * rows, width), dtype),
        ],
        in_specs=[pl.BlockSpec(memory_space=pltpu.VMEM)] * len(pieces),
        out_specs=[pl.BlockSpec(memory_space=pl.ANY), pl.BlockSpec(memory_space=pltpu.VMEM)],
        scratch_shapes=[pltpu.SemaphoreType.DMA((len(CHIPS),))],
        compiler_params=pltpu.CompilerParams(vmem_limit_bytes=8 << 20),
        cost_estimate=pl.CostEstimate(flops=0, bytes_accessed=4 * sum(p.size for p in pieces), transcendentals=0),
    )(*pieces)


def send(piece, groups, hop):
    if hop == (0, 0):
        return piece
    pairs = [(i, (i // 2 + hop[0]) % (groups // 2) * 2 + (i + hop[1]) % 2) for i in range(groups)]
    return lax.ppermute(piece, "el", pairs)


def on_device(field_points, owner_map, send_counts, tile_rows, tile_cols, weights):
    elems, points, channels = field_points.shape
    devices = lax.axis_size(("el", "tg"))
    groups = lax.axis_size("el")
    packed = pack(owner_map, send_counts, field_points)
    outgoing = packed.reshape(devices, elems // devices * points, channels)
    incoming = lax.all_to_all(outgoing, ("el", "tg"), split_axis=0, concat_axis=0, tiled=True)
    ready = stage(tile_rows, weights)
    source = incoming.reshape(-1, weights.shape[-1], channels)
    targets, tile = weights.shape[1], weights.shape[-1]
    count = targets * SHARES[0] // sum(SHARES)
    *pieces, source = remap(0, count, True, tile_rows, tile_cols, weights, source, ready)
    received = [send(piece, groups, hop) for piece, hop in zip(pieces, HOPS_OF[True])]
    pieces = remap(count, targets - count, False, tile_rows, tile_cols, weights, source)
    whole, away = split(0, targets * tile, groups, received)
    away = send(away, groups, (0, 1))
    received = [send(piece, groups, hop) for piece, hop in zip(pieces, HOPS)]
    whole = join(0, tuple((chip, 1) for chip in CHIPS), groups, [away], whole)
    whole = join(count * tile, tuple(HOPS[n] for n in EARLY), groups, [received[n] for n in EARLY], whole)
    whole = join(count * tile, tuple(HOPS[n] for n in LATE), groups, [received[n] for n in LATE], whole)
    return whole


def solution(mesh):
    return jax.shard_map(
        on_device,
        mesh=mesh,
        in_specs=(
            P(("el", "tg"), None, None),
            P(("el", "tg"), None),
            P(("el", "tg"), None),
            P(("el", "tg"), None),
            P(("el", "tg"), None, None),
            P(("el", "tg"), None, None, None, None),
        ),
        out_specs=P("el", "tg"),
        check_vma=False,
    )
```

```python
import functools

import jax
import jax.numpy as jnp
from jax import lax
from jax.experimental import pallas as pl
from jax.experimental.pallas import tpu as pltpu
from jax.sharding import PartitionSpec as P

SHARES = (7, 9)
STAGED = 6
CHIPS = (1, 3, 2, 0)
EARLY = (0, 1, 2, 3, 6, 7)
LATE = (4, 5)
GROUP = 4
AHEAD = 2
HOPS = ((1, 0), (3, 0), (2, 0), (2, 1), (1, 1), (3, 1), (0, 1), (0, 0))


def pack_kernel(chunks, owner_ref, counts_ref, field_ref, out_ref, buf, dst, pos_v, pos_s, sem_in, sem_pos, sem_out):
    elems, points, channels = dst.shape
    step = elems // chunks
    owners = elems // 4

    def fetch(c):
        return pltpu.make_async_copy(field_ref.at[pl.ds(c * step, step)], buf.at[pl.ds(c * step, step)], sem_in.at[c])

    for c in range(chunks):
        fetch(c).start()
    owner = owner_ref[...]
    hit = lax.broadcasted_iota(jnp.int32, (owners, elems), 0) == owner
    hit = jnp.where(hit, 1.0, 0.0)
    before = jnp.where(lax.broadcasted_iota(jnp.int32, (elems, elems), 0) < lax.broadcasted_iota(jnp.int32, (elems, elems), 1), 1.0, 0.0)
    earlier = jnp.dot(hit.astype(jnp.bfloat16), before.astype(jnp.bfloat16), preferred_element_type=jnp.float32)
    rank = jnp.sum(hit * earlier, axis=0, keepdims=True)
    pos_v[...] = owner * 4 + rank.astype(jnp.int32)
    cp = pltpu.make_async_copy(pos_v, pos_s, sem_pos)
    cp.start()
    cp.wait()
    point = lax.broadcasted_iota(jnp.int32, (points, channels), 0)
    for c in range(chunks):
        fetch(c).wait()

        def body(e, carry):
            live = point < counts_ref[0, e]
            dst[pos_s[0, e]] = jnp.where(live, buf[e], jnp.zeros((), buf.dtype))
            return carry

        lax.fori_loop(c * step, (c + 1) * step, body, 0, unroll=8)
    out = pltpu.make_async_copy(dst, out_ref, sem_out)
    out.start()
    out.wait()


def pack(owner_map, send_counts, field, chunks=8):
    return pl.pallas_call(
        functools.partial(pack_kernel, chunks),
        out_shape=jax.ShapeDtypeStruct(field.shape, field.dtype),
        in_specs=[pl.BlockSpec(memory_space=pltpu.VMEM), pl.BlockSpec(memory_space=pltpu.SMEM), pl.BlockSpec(memory_space=pl.ANY)],
        out_specs=pl.BlockSpec(memory_space=pl.ANY),
        scratch_shapes=[
            pltpu.VMEM(field.shape, field.dtype),
            pltpu.VMEM(field.shape, field.dtype),
            pltpu.VMEM((1, field.shape[0]), jnp.int32),
            pltpu.SMEM((1, field.shape[0]), jnp.int32),
            pltpu.SemaphoreType.DMA((chunks,)),
            pltpu.SemaphoreType.DMA,
            pltpu.SemaphoreType.DMA,
        ],
        name="pack",
    )(owner_map, send_counts, field)


HOPS_OF = {False: HOPS, True: tuple((chip, 0) for chip in CHIPS)}


def peer(me, groups, hop):
    chip, core = me // 2, me % 2
    return lax.rem(chip + hop[0], groups // 2) * 2 + (1 - core if hop[1] else core)


def stage_kernel(rows_ref, w_ref, out_ref, order, sems):
    for t in range(rows_ref.shape[1]):
        order[rows_ref[0, t]] = t
    copies = [pltpu.make_async_copy(w_ref.at[0, order[q]], out_ref.at[q], sems.at[q]) for q in range(STAGED)]
    for copy in copies:
        copy.start()
    for copy in copies:
        copy.wait()


def stage(tile_rows, weights):
    return pl.pallas_call(
        stage_kernel,
        out_shape=jax.ShapeDtypeStruct((STAGED, *weights.shape[2:]), weights.dtype),
        in_specs=[pl.BlockSpec(memory_space=pltpu.SMEM), pl.BlockSpec(memory_space=pl.ANY)],
        out_specs=pl.BlockSpec(memory_space=pltpu.VMEM),
        scratch_shapes=[pltpu.SMEM(tile_rows.shape[1:], jnp.int32), pltpu.SemaphoreType.DMA((STAGED,))],
        compiler_params=pltpu.CompilerParams(vmem_limit_bytes=46 << 20),
        cost_estimate=pl.CostEstimate(flops=0, bytes_accessed=4 * STAGED * weights[0, 0].size, transcendentals=0),
        name="stage",
    )(tile_rows, weights)


def remap_kernel(first, staged, paired, axis, rows_ref, cols_ref, w_ref, src_ref, *refs):
    outs, (w_buf, out, order, sem_src, sem_w) = list(refs[staged > 0 : -5]), refs[-5:]
    src = src_ref
    _, targets, blocks, tile, _ = w_ref.shape
    count = out.shape[1] // tile
    groups = len(HOPS)
    rows = out.shape[0] // groups
    if staged:
        src = outs.pop()
        load = pltpu.make_async_copy(src_ref, src, sem_src)
        load.start()
    for t in range(targets):
        order[rows_ref[0, t]] = t

    def fetch(q):
        return pltpu.make_async_copy(w_ref.at[0, order[first + q]], w_buf.at[q - staged], sem_w.at[q - staged])

    def block(q, k):
        return refs[0][q, k] if q < staged else w_buf[q - staged, k]

    for q in range(staged, GROUP * AHEAD):
        fetch(q).start()
    me = lax.axis_index(axis) if axis else 0
    places = [peer(me, groups, hop) // 2 * 2 if paired else peer(me, groups, hop) for hop in HOPS_OF[paired]]

    def hand_out(g):
        lanes = slice(g * tile, min(count, g + GROUP) * tile)
        for piece, row in zip(outs, places):
            piece[:, lanes] = out[pl.ds(pl.multiple_of(row * rows, rows), piece.shape[0]), lanes]

    if staged:
        load.wait()
    for g in range(0, count, GROUP):
        for q in range(max(g, staged), min(count, g + GROUP)):
            fetch(q).wait()
        for q in range(g + GROUP * AHEAD, min(count, g + GROUP * AHEAD + GROUP)):
            fetch(q).start()
        if g:
            hand_out(g - GROUP)
        for q in range(g, min(count, g + GROUP)):
            t = order[first + q]
            total = None
            for k in range(0, blocks, 2):
                w = jnp.concatenate([block(q, k), block(q, k + 1)], axis=1)
                x = jnp.concatenate([src[cols_ref[0, t, k]], src[cols_ref[0, t, k + 1]]], axis=0)
                r = jnp.dot(w, x, preferred_element_type=jnp.float32)
                total = r if total is None else total + r
            out[:, q * tile : (q + 1) * tile] = total.T.astype(out.dtype)
    hand_out(count - 1 - (count - 1) % GROUP)


def remap(first, count, paired, tile_rows, tile_cols, weights, source, ready=None, axis="el"):
    _, targets, blocks, tile, _ = weights.shape
    channels = source.shape[-1]
    staged = 0 if ready is None else STAGED
    pieces = len(HOPS_OF[paired])
    shapes = [jax.ShapeDtypeStruct((channels // pieces, count * tile), source.dtype)] * pieces
    vmem = pl.BlockSpec(memory_space=pltpu.VMEM)
    held = [pl.BlockSpec(memory_space=pl.ANY), vmem] if staged else [vmem]
    if staged:
        shapes.append(jax.ShapeDtypeStruct(source.shape, source.dtype))
    return pl.pallas_call(
        functools.partial(remap_kernel, first, staged, paired, axis),
        out_shape=shapes,
        in_specs=[pl.BlockSpec(memory_space=pltpu.SMEM)] * 2 + [pl.BlockSpec(memory_space=pl.ANY)] + held,
        out_specs=[vmem] * len(shapes),
        scratch_shapes=[
            pltpu.VMEM((count - staged, *weights.shape[2:]), weights.dtype),
            pltpu.VMEM((channels, count * tile), source.dtype),
            pltpu.SMEM((targets,), jnp.int32),
            pltpu.SemaphoreType.DMA,
            pltpu.SemaphoreType.DMA((count - staged,)),
        ],
        compiler_params=pltpu.CompilerParams(vmem_limit_bytes=46 << 20),
        cost_estimate=pl.CostEstimate(
            flops=2 * count * blocks * tile * tile * channels,
            bytes_accessed=2 * (weights.size * count // targets + source.size),
            transcendentals=0,
        ),
    )(tile_rows, tile_cols, weights, source, *([ready] if staged else []))


def place(me, groups, start, piece, hop, out_ref, sem):
    chip, core = hop
    source = peer(me, groups, ((groups // 2 - chip) % (groups // 2), core))
    lane = pl.multiple_of(source * (out_ref.shape[1] // groups) + start, 128)
    return pltpu.make_async_copy(piece, out_ref.at[:, pl.ds(lane, piece.shape[1])], sem)


def join_kernel(start, groups, hops, axis, *refs):
    out_ref, sems = refs[-2:]
    me = lax.axis_index(axis) if axis else 0
    rows = out_ref.shape[0]
    stores = []
    for i, hop in enumerate(hops):
        piece = refs[i] if len(refs) > 4 else refs[0].at[pl.ds(i * rows, rows)]
        stores.append(place(me, groups, start, piece, hop, out_ref, sems.at[i]))
        stores[i].start()
    for store in stores:
        store.wait()


def join(start, hops, groups, pieces, whole, axis="el"):
    return pl.pallas_call(
        functools.partial(join_kernel, start, groups, hops, axis),
        out_shape=jax.ShapeDtypeStruct(whole.shape, whole.dtype),
        in_specs=[pl.BlockSpec(memory_space=pltpu.VMEM)] * len(pieces) + [pl.BlockSpec(memory_space=pl.ANY)],
        out_specs=pl.BlockSpec(memory_space=pl.ANY),
        scratch_shapes=[pltpu.SemaphoreType.DMA((len(hops),))],
        input_output_aliases={len(pieces): 0},
        compiler_params=pltpu.CompilerParams(vmem_limit_bytes=8 << 20),
        cost_estimate=pl.CostEstimate(flops=0, bytes_accessed=4 * sum(p.size for p in pieces), transcendentals=0),
    )(*pieces, whole)


def split_kernel(start, groups, axis, *refs):
    pieces, (out_ref, away_ref, sems) = refs[: len(CHIPS)], refs[-3:]
    me = lax.axis_index(axis) if axis else 0
    core = me % 2
    rows = out_ref.shape[0]
    stores = []
    for i, chip in enumerate(CHIPS):
        kept = pieces[i].at[pl.ds(pl.multiple_of(core * rows, rows), rows)]
        stores.append(place(me, groups, start, kept, (chip, 0), out_ref, sems.at[i]))
        stores[i].start()
    for i in range(len(CHIPS)):
        away_ref[i * rows : (i + 1) * rows] = pieces[i][pl.ds(pl.multiple_of((1 - core) * rows, rows), rows)]
    for store in stores:
        store.wait()


def split(start, span, groups, pieces, axis="el"):
    rows, width = pieces[0].shape[0] // 2, pieces[0].shape[1]
    dtype = pieces[0].dtype
    return pl.pallas_call(
        functools.partial(split_kernel, start, groups, axis),
        out_shape=[
            jax.ShapeDtypeStruct((rows, groups * span), dtype),
            jax.ShapeDtypeStruct((len(CHIPS) * rows, width), dtype),
        ],
        in_specs=[pl.BlockSpec(memory_space=pltpu.VMEM)] * len(pieces),
        out_specs=[pl.BlockSpec(memory_space=pl.ANY), pl.BlockSpec(memory_space=pltpu.VMEM)],
        scratch_shapes=[pltpu.SemaphoreType.DMA((len(CHIPS),))],
        compiler_params=pltpu.CompilerParams(vmem_limit_bytes=8 << 20),
        cost_estimate=pl.CostEstimate(flops=0, bytes_accessed=4 * sum(p.size for p in pieces), transcendentals=0),
    )(*pieces)


def send(piece, groups, hop):
    if hop == (0, 0):
        return piece
    pairs = [(i, (i // 2 + hop[0]) % (groups // 2) * 2 + (i + hop[1]) % 2) for i in range(groups)]
    return lax.ppermute(piece, "el", pairs)


def on_device(field_points, owner_map, send_counts, tile_rows, tile_cols, weights):
    elems, points, channels = field_points.shape
    devices = lax.axis_size(("el", "tg"))
    groups = lax.axis_size("el")
    packed = pack(owner_map, send_counts, field_points)
    outgoing = packed.reshape(devices, elems // devices * points, channels)
    incoming = lax.all_to_all(outgoing, ("el", "tg"), split_axis=0, concat_axis=0, tiled=True)
    ready = stage(tile_rows, weights)
    source = incoming.reshape(-1, weights.shape[-1], channels)
    targets, tile = weights.shape[1], weights.shape[-1]
    count = targets * SHARES[0] // sum(SHARES)
    *pieces, source = remap(0, count, True, tile_rows, tile_cols, weights, source, ready)
    received = [send(piece, groups, hop) for piece, hop in zip(pieces, HOPS_OF[True])]
    pieces = remap(count, targets - count, False, tile_rows, tile_cols, weights, source)
    whole, away = split(0, targets * tile, groups, received)
    away = send(away, groups, (0, 1))
    received = [send(piece, groups, hop) for piece, hop in zip(pieces, HOPS)]
    whole = join(0, tuple((chip, 1) for chip in CHIPS), groups, [away], whole)
    whole = join(count * tile, tuple(HOPS[n] for n in EARLY), groups, [received[n] for n in EARLY], whole)
    whole = join(count * tile, tuple(HOPS[n] for n in LATE), groups, [received[n] for n in LATE], whole)
    return whole


def solution(mesh):
    return jax.shard_map(
        on_device,
        mesh=mesh,
        in_specs=(
            P(("el", "tg"), None, None),
            P(("el", "tg"), None),
            P(("el", "tg"), None),
            P(("el", "tg"), None),
            P(("el", "tg"), None, None),
            P(("el", "tg"), None, None, None, None),
        ),
        out_specs=P("el", "tg"),
        check_vma=False,
    )
```
